32 devices in a mesh: dp: 8 (over z, y), section: 4 (over x, core).
Axes of the slice: x: 2, y: 2, z: 4, core: 2. Of those that a mesh axis runs over, the one named last changes fastest.
Arguments:
- patches: bfloat16 [64, 197, 1024], P('dp'), may hold values from -6 to 6
- ln1_gain: float32 [4, 1024], P('section'), may hold values from 0.5 to 1.5
- w_qkv: bfloat16 [4, 1024, 3072], P('section'), may hold values from -1 to 1
- w_out: bfloat16 [4, 1024, 1024], P('section'), may hold values from -0.1875 to 0.1875
- ln2_gain: float32 [4, 1024], P('section'), may hold values from 0.5 to 1.5
- w_fc1: bfloat16 [4, 1024, 2048], P('section'), may hold values from -0.1875 to 0.1875
- w_fc2: bfloat16 [4, 2048, 1024], P('section'), may hold values from -0.125 to 0.125
- final_norm_gain: float32 [1024], replicated, may hold values from 0.5 to 1.5
- w_head: bfloat16 [1024, 256], replicated, may hold values from -0.1875 to 0.1875
- online_embeddings: bfloat16 [64, 256], P('dp'), may hold values from -60 to 60
- queue: bfloat16 [32768, 256], P(('dp', 'section')), may hold values from -1 to 1, as said below
- owner: int32 [64], replicated, may hold values from 0 to 63, each once
- pointer: int32 [8], P('dp'), may hold values from 0 to 4088
Outputs:
- momentum_embeddings: bfloat16 [64, 256], P('dp')
- query_loss: float32 [64], P('dp')
- total_loss: float32 [], replicated
- new_queue: bfloat16 [32768, 256], P(('dp', 'section'))
The draws below stay inside these ranges and needn't reach their ends.
Inputs may be any that keep to these rules, and one draw needn't show every extreme that they name: `queue`: every row has Euclidean norm below 1. Each value appears once: key j goes to group owner[j] // 8, so every group receives exactly 8 keys. `pointer`: first row of the group's shard where its new keys are written.
All inputs are finite; a program needn't handle non-finite values.
Results may differ from the reference program's by a relative error of at most 0.02.
Values may be sent and summed in bfloat16 or wider, within the bound.
A program may use at most 128 MiB of HBM per device.

```python
import math
import jax
import jax.numpy as jnp
from jax import lax

D = 1024
HEADS = 16
HEAD_DIM = 64
FF = 2048
TOKS = 197
KDIM = 256
Q_GROUP = 4096
IMG_GROUP = 8
IMAGES = 64
QROWS = 32768
N_DP = 8
N_SECTION = 4


def draw_w_qkv(key, part):
    result = jax.random.normal(jax.random.fold_in(key, 23), (N_SECTION, D, 3 * D), jnp.float32) / D ** 0.5
    result = jnp.clip(result, -6.0 / D ** 0.5, 6.0 / D ** 0.5)
    return result.astype(jnp.bfloat16)


def queue_rows(key):
    sample_count = jax.random.normal(jax.random.fold_in(key, 11), (QROWS, KDIM), jnp.float32)
    return sample_count * jax.lax.rsqrt(jnp.sum(sample_count * sample_count, axis=1, keepdims=True) + 1.0)


def draw_queue(key, part):
    return queue_rows(key).astype(jnp.bfloat16)


def draw_online_embeddings(key, part):
    result = jnp.clip(jax.random.normal(jax.random.fold_in(key, 5), (IMAGES, KDIM), jnp.float32), -6.0, 6.0)
    return result.astype(jnp.bfloat16)


def plant(drawn, key, low, largest):
    place = [jax.random.randint(jax.random.fold_in(key, axis), (), 0, length) for axis, length in enumerate(drawn.shape)]
    main_axis = drawn.shape.index(max(drawn.shape))
    beside = place[:main_axis] + [(place[main_axis] + 1) % drawn.shape[main_axis]] + place[main_axis + 1:]
    return drawn.at[tuple(place)].set(low).at[tuple(beside)].set(largest)


def block_levels(key, shape, cuts, least, top_value):
    level = 1.0
    for position, blocks in cuts:
        heights = jax.random.uniform(jax.random.fold_in(jax.random.fold_in(key, 6), position), (blocks,), jnp.float32, least / len(cuts), top_value / len(cuts))
        level = level * jnp.repeat(jnp.exp(heights), shape[position] // blocks).reshape((-1,) + (1,) * (len(shape) - 1 - position))
    return level


def scatter_about(key, dims, scale, limit, cuts=(), kind=jnp.bfloat16):
    loudness = block_levels(key, dims, cuts, -0.22, 0.18) if cuts else 1.0
    array = jax.random.normal(key, dims, jnp.float32) * scale * loudness
    return jnp.minimum(jnp.maximum(array, -limit), limit).astype(kind)


def setup_inputs(seed: int = 0) -> dict:
    seeds = jax.random.split(jax.random.key(seed), 14)
    return {
        "patches": scatter_about(seeds[0], (IMAGES, TOKS, D), 1.0, 6.0, ((0, 8),)),
        "ln1_gain": jnp.clip(1.0 + 0.1 * jax.random.normal(seeds[1], (N_SECTION, D), jnp.float32), 0.5, 1.5),
        "w_qkv": draw_w_qkv(jax.random.fold_in(seeds[13], 71), 0),
        "w_out": scatter_about(seeds[3], (N_SECTION, D, D), D ** -0.5, 0.1875, ((0, 4),)),
        "ln2_gain": jnp.clip(1.0 + 0.1 * jax.random.normal(seeds[4], (N_SECTION, D), jnp.float32), 0.5, 1.5),
        "w_fc1": scatter_about(seeds[5], (N_SECTION, D, FF), D ** -0.5, 0.1875, ((0, 4),)),
        "w_fc2": scatter_about(seeds[6], (N_SECTION, FF, D), FF ** -0.5, 0.125, ((0, 4),)),
        "final_norm_gain": jnp.clip(1.0 + 0.1 * jax.random.normal(seeds[7], (D,), jnp.float32), 0.5, 1.5),
        "w_head": scatter_about(seeds[8], (D, KDIM), D ** -0.5, 0.1875),
        "online_embeddings": draw_online_embeddings(jax.random.fold_in(seeds[13], 71), 0),
        "queue": draw_queue(jax.random.fold_in(seeds[13], 71), 0),
        "owner": jax.random.permutation(seeds[11], IMAGES).astype(jnp.int32),
        "pointer": plant(jax.random.randint(seeds[12], (N_DP,), 0, Q_GROUP - IMG_GROUP + 1), jax.random.fold_in(seeds[12], 1), 0, Q_GROUP - IMG_GROUP).astype(jnp.int32),
    }


contrastive_sharpness = 0.2

def layer_norm(values, gain):
    center = values - lax.optimization_barrier(jnp.mean(values, axis=-1, keepdims=True))
    spread = lax.optimization_barrier(jnp.mean(center * center, axis=-1, keepdims=True))
    return center * lax.rsqrt(spread + 1e-06) * gain

def cycle_buffer(values):
    return lax.optimization_barrier(values.astype(jnp.bfloat16)).astype(jnp.float32)

def encoder_block(hidden, gain_one, qkv_weight, out_weight, gain_two, first_weight, second_weight):
    images = hidden.shape[0]
    width = hidden.shape[2]
    stream = hidden.astype(jnp.float32)
    normed = layer_norm(stream, gain_one).astype(jnp.bfloat16).reshape(images * TOKS, width)
    packed = jnp.dot(normed, qkv_weight, preferred_element_type=jnp.float32)
    packed = cycle_buffer(packed).reshape(images, TOKS, 3, HEADS, HEAD_DIM)
    similarity_matrix = jnp.einsum('bqhd,bkhd->bhqk', packed[:, :, 0], packed[:, :, 1]) / math.sqrt(HEAD_DIM)
    peak = lax.optimization_barrier(jnp.max(similarity_matrix, axis=-1, keepdims=True))
    expo = jnp.exp(similarity_matrix - peak)
    probs = cycle_buffer(expo / lax.optimization_barrier(jnp.sum(expo, axis=-1, keepdims=True)))
    context = jnp.einsum('bhqk,bkhd->bqhd', probs, packed[:, :, 2])
    context = context.astype(jnp.bfloat16).reshape(images * TOKS, width)
    stream = stream + jnp.dot(context, out_weight, preferred_element_type=jnp.float32).reshape(images, TOKS, width)
    normed = layer_norm(stream, gain_two).astype(jnp.bfloat16).reshape(images * TOKS, width)
    inner = jax.nn.gelu(jnp.dot(normed, first_weight, preferred_element_type=jnp.float32), approximate=False)
    inner = inner.astype(jnp.bfloat16)
    stream = stream + jnp.dot(inner, second_weight, preferred_element_type=jnp.float32).reshape(images, TOKS, width)
    return stream.astype(jnp.bfloat16)

def key_head(class_rows, final_norm_gain, w_head):
    normed = layer_norm(class_rows.astype(jnp.float32), final_norm_gain).astype(jnp.bfloat16)
    projected = jnp.dot(normed, w_head, preferred_element_type=jnp.float32)
    scale = lax.rsqrt(1.0 + lax.optimization_barrier(jnp.sum(projected * projected, axis=1, keepdims=True)))
    return (projected * scale).astype(jnp.bfloat16)

def reference(patches, ln1_gain, w_qkv, w_out, ln2_gain, w_fc1, w_fc2, final_norm_gain, w_head, online_embeddings, queue, owner, pointer):

    def encode_group(images):
        hidden = images
        for layer_section in range(N_SECTION):
            hidden = encoder_block(hidden, ln1_gain[layer_section], w_qkv[layer_section], w_out[layer_section], ln2_gain[layer_section], w_fc1[layer_section], w_fc2[layer_section])
        return key_head(hidden[:, 0, :], final_norm_gain, w_head)
    momentum_embeddings = lax.map(encode_group, patches.reshape(N_DP, IMG_GROUP, TOKS, D)).reshape(IMAGES, KDIM)
    matching_similarity = lax.optimization_barrier(jnp.sum(online_embeddings.astype(jnp.float32) * momentum_embeddings.astype(jnp.float32), axis=1)) / contrastive_sharpness

    def score_group(sample_count):
        similarity_matrix = jnp.dot(online_embeddings, sample_count.T, preferred_element_type=jnp.float32) / contrastive_sharpness
        peak = lax.optimization_barrier(jnp.max(similarity_matrix, axis=1))
        return (peak, lax.optimization_barrier(jnp.sum(jnp.exp(similarity_matrix - peak[:, None]), axis=1)))
    peaks, totals = lax.map(score_group, queue.reshape(N_DP, Q_GROUP, KDIM))
    top = lax.optimization_barrier(jnp.max(peaks, axis=0))
    negative = top + jnp.log(lax.optimization_barrier(jnp.sum(totals * jnp.exp(peaks - top[None, :]), axis=0)))
    larger = jnp.maximum(negative, matching_similarity)
    query_loss = larger + jnp.log(jnp.exp(negative - larger) + jnp.exp(matching_similarity - larger)) - matching_similarity
    total_loss = jnp.sum(query_loss) / IMAGES
    order = jnp.zeros((IMAGES,), jnp.int32).at[owner].set(jnp.arange(IMAGES, dtype=jnp.int32))
    entries = momentum_embeddings[order].reshape(N_DP, IMG_GROUP, KDIM)

    def enqueue(pieces):
        sample_count, fresh, start = pieces
        return lax.dynamic_update_slice_in_dim(sample_count, fresh, start.astype(jnp.int32), 0)
    new_queue = lax.map(enqueue, (queue.reshape(N_DP, Q_GROUP, KDIM), entries, pointer)).reshape(QROWS, KDIM)
    return (momentum_embeddings, query_loss, total_loss, new_queue)
```

```python
import functools
import math

import jax
import jax.numpy as jnp
from jax import lax
from jax.experimental import pallas as pl
from jax.experimental.pallas import tpu as pltpu
from jax.sharding import PartitionSpec as P

HEAD_DIM = 64


contrastive_sharpness = 0.2


def broadcast(value, axis, source):
    kept = jnp.where(lax.axis_index(axis) == source, value, 0).astype(value.dtype)
    return lax.psum(kept, axis)


def layer_norm(values, gain):
    center = values - jnp.mean(values, axis=-1, keepdims=True)
    spread = jnp.mean(center * center, axis=-1, keepdims=True)
    return center * lax.rsqrt(spread + 1e-06) * gain


def rounded_up(value, step):
    return (value + step - 1) // step * step


def gelu(x):
    return 0.5 * x * (1.0 + lax.erf(x * math.sqrt(0.5)))


def column_loop(total, tile, body):
    @pl.loop(0, total // tile)
    def _(step):
        body(pl.ds(pl.multiple_of(step * tile, tile), tile))


def attend(qkv_buf, c_buf, toks, width):
    rows = c_buf.shape[0]
    pair = 2 * HEAD_DIM
    lane = lax.broadcasted_iota(jnp.int32, (rows, pair), 1)
    first = lane < HEAD_DIM
    key_place = lax.broadcasted_iota(jnp.int32, (2 * rows, rows), 1)
    factor = math.log2(math.e) / math.sqrt(HEAD_DIM)

    def one_pair(columns, k_columns, v_columns):
        q = qkv_buf[:, columns]
        zero = jnp.zeros_like(q)
        q_both = jnp.concatenate([jnp.where(first, q, zero), jnp.where(first, zero, q)], axis=0)
        k = qkv_buf[:, k_columns]
        scores = lax.dot_general(
            q_both, k, (((1,), (1,)), ((), ())), preferred_element_type=jnp.float32
        )
        scores = jnp.where(key_place < toks, scores, -jnp.inf)
        peak = jnp.max(scores, axis=1, keepdims=True)
        expo = jnp.exp2((scores - peak) * factor)
        total = jnp.sum(expo, axis=1, keepdims=True)
        c = jnp.dot(
            expo.astype(jnp.bfloat16), qkv_buf[:, v_columns], preferred_element_type=jnp.float32
        )
        c = c / total
        c_buf[:, columns] = jnp.where(first, c[:rows], c[rows:]).astype(jnp.bfloat16)

    for at in range(0, width, pair):
        one_pair(
            pl.ds(at, pair),
            pl.ds(width + at, pair),
            pl.ds(2 * width + at, pair),
        )


def pipeline_kernel(
    sections,
    toks,
    patches,
    gain_one,
    gain_two,
    w_qkv,
    w_out,
    w_fc1,
    w_fc2,
    class_rows,
    v_qkv,
    v_out,
    v_fc1,
    v_fc2,
    raw,
    came,
    leaving,
    a_buf,
    qkv_buf,
    c_buf,
    r_buf,
    u_buf,
    weight_sem,
    raw_sem,
    send_sem,
    recv_sem,
):
    me = lax.axis_index("section")
    images, rows, width = came.shape
    hidden_units = v_fc1.shape[1]
    loads = [
        pltpu.make_async_copy(source.at[0], target, weight_sem.at[place])
        for place, (source, target) in enumerate(
            ((w_qkv, v_qkv), (w_out, v_out), (w_fc1, v_fc1), (w_fc2, v_fc2))
        )
    ]

    def raw_load(image):
        return pltpu.make_async_copy(patches.at[image], raw.at[image], raw_sem.at[image])

    @pl.when(me == 0)
    def _():
        raw_load(0).start()

    loads[0].start()
    for load in loads[1:]:
        load.start()

    @pl.when(me == 0)
    def _():
        for image in range(1, images):
            raw_load(image).start()

    barrier = pltpu.get_barrier_semaphore()

    @pl.when(me > 0)
    def _():
        pl.semaphore_signal(
            barrier, inc=1, device_id={"section": me - 1}, device_id_type=pl.DeviceIdType.MESH
        )

    @pl.when(me < sections - 1)
    def _():
        pl.semaphore_signal(
            barrier, inc=1, device_id={"section": me + 1}, device_id_type=pl.DeviceIdType.MESH
        )

    inner = jnp.logical_and(me > 0, me < sections - 1)

    @pl.when(inner)
    def _():
        pl.semaphore_wait(barrier, 2)

    @pl.when(jnp.logical_not(inner))
    def _():
        pl.semaphore_wait(barrier, 1)

    def handing(image):
        return pltpu.make_async_remote_copy(
            src_ref=leaving.at[image],
            dst_ref=came.at[image],
            send_sem=send_sem.at[image],
            recv_sem=recv_sem.at[image],
            device_id={"section": jnp.minimum(me + 1, sections - 1)},
            device_id_type=pl.DeviceIdType.MESH,
        )

    @pl.loop(0, images)
    def _(image):
        @pl.when(me == 0)
        def _():
            raw_load(image).wait()
            came[image, toks // 16 * 16 :, :] = jnp.zeros(
                (rows - toks // 16 * 16, width), jnp.bfloat16
            )
            came[image, 0:toks, :] = raw[image]

        @pl.when(me > 0)
        def _():
            handing(image).wait_recv()

        def arrive(place):
            @pl.when(image == 0)
            def _():
                loads[place].wait()

        a_buf[...] = layer_norm(came[image].astype(jnp.float32), gain_one[...]).astype(jnp.bfloat16)
        arrive(0)

        def qkv_part(columns):
            qkv_buf[:, columns] = jnp.dot(
                a_buf[...], v_qkv[:, columns], preferred_element_type=jnp.float32
            ).astype(jnp.bfloat16)

        column_loop(3 * width, 512, qkv_part)
        attend(qkv_buf, c_buf, toks, width)
        arrive(1)

        def out_part(columns):
            r_buf[:, columns] = came[image, :, columns].astype(jnp.float32) + jnp.dot(
                c_buf[...], v_out[:, columns], preferred_element_type=jnp.float32
            )

        column_loop(width, 512, out_part)
        a_buf[...] = layer_norm(r_buf[...], gain_two[...]).astype(jnp.bfloat16)
        arrive(2)

        def fc1_part(columns):
            u_buf[:, columns] = gelu(
                jnp.dot(a_buf[...], v_fc1[:, columns], preferred_element_type=jnp.float32)
            ).astype(jnp.bfloat16)

        column_loop(hidden_units, 512, fc1_part)
        arrive(3)

        def fc2_part(columns):
            leaving[image, :, columns] = (
                r_buf[:, columns]
                + jnp.dot(u_buf[...], v_fc2[:, columns], preferred_element_type=jnp.float32)
            ).astype(jnp.bfloat16)

        column_loop(width, 512, fc2_part)

        @pl.when(me < sections - 1)
        def _():
            handing(image).start()

    for image in range(images):
        class_rows[image : image + 1, :] = leaving[image, 0:1, :]

    @pl.when(me < sections - 1)
    def _():
        for image in range(images):
            handing(image).wait_send()


def run_pipeline(patches, gain_one, w_qkv, w_out, gain_two, w_fc1, w_fc2):
    sections = lax.axis_size("section")
    images, toks, width = patches.shape
    rows = rounded_up(toks, 16)
    hidden_units = w_fc1.shape[2]
    bf16 = jnp.bfloat16
    whole = pl.BlockSpec(memory_space=pltpu.VMEM)
    hbm = pl.BlockSpec(memory_space=pl.ANY)
    flops = 2 * images * toks * (4 * width * width + 2 * width * hidden_units)
    return pl.pallas_call(
        functools.partial(pipeline_kernel, sections, toks),
        out_shape=jax.ShapeDtypeStruct((images, width), bf16),
        in_specs=[hbm, whole, whole, hbm, hbm, hbm, hbm],
        out_specs=whole,
        scratch_shapes=[
            pltpu.VMEM((width, 3 * width), bf16),
            pltpu.VMEM((width, width), bf16),
            pltpu.VMEM((width, hidden_units), bf16),
            pltpu.VMEM((hidden_units, width), bf16),
            pltpu.VMEM((images, toks, width), bf16),
            pltpu.VMEM((images, rows, width), bf16),
            pltpu.VMEM((images, rows, width), bf16),
            pltpu.VMEM((rows, width), bf16),
            pltpu.VMEM((rows, 3 * width), bf16),
            pltpu.VMEM((rows, width), bf16),
            pltpu.VMEM((rows, width), jnp.float32),
            pltpu.VMEM((rows, hidden_units), bf16),
            pltpu.SemaphoreType.DMA((4,)),
            pltpu.SemaphoreType.DMA((images,)),
            pltpu.SemaphoreType.DMA((images,)),
            pltpu.SemaphoreType.DMA((images,)),
        ],
        compiler_params=pltpu.CompilerParams(
            collective_id=0, has_side_effects=True, vmem_limit_bytes=52 * 1024 * 1024
        ),
        cost_estimate=pl.CostEstimate(flops=flops, bytes_accessed=2**24, transcendentals=2**22),
    )(patches, gain_one, gain_two, w_qkv, w_out, w_fc1, w_fc2)


def key_head(class_rows, final_norm_gain, w_head):
    normed = layer_norm(class_rows.astype(jnp.float32), final_norm_gain).astype(jnp.bfloat16)
    projected = jnp.dot(normed, w_head, preferred_element_type=jnp.float32)
    scale = lax.rsqrt(1.0 + jnp.sum(projected * projected, axis=1, keepdims=True))
    return (projected * scale).astype(jnp.bfloat16)


def on_device(
    patches,
    ln1_gain,
    w_qkv,
    w_out,
    ln2_gain,
    w_fc1,
    w_fc2,
    final_norm_gain,
    w_head,
    online_embeddings,
    queue,
    owner,
    pointer,
):
    sections = lax.axis_size("section")
    section_index = lax.axis_index("section")
    group_index = lax.axis_index("dp")
    group_images = patches.shape[0]
    finished = run_pipeline(patches, ln1_gain, w_qkv, w_out, ln2_gain, w_fc1, w_fc2)
    resident_embeddings = key_head(finished, final_norm_gain, w_head)
    momentum_embeddings = broadcast(resident_embeddings, "section", sections - 1)
    query_rows_full = lax.all_gather(online_embeddings, "dp", axis=0, tiled=True)
    share = queue.shape[0]
    similarity_matrix = (
        jnp.einsum("tw,fw->tf", query_rows_full, queue, preferred_element_type=jnp.float32)
        / contrastive_sharpness
    )
    local_peak = jnp.max(similarity_matrix, axis=1)
    top = lax.pmax(local_peak, ("dp", "section"))
    total = lax.psum(jnp.sum(jnp.exp(similarity_matrix - top[:, None]), axis=1), ("dp", "section"))
    negative_all = top + jnp.log(total)
    negative = lax.dynamic_slice_in_dim(negative_all, group_index * group_images, group_images, 0)
    matching_similarity = (
        jnp.sum(
            online_embeddings.astype(jnp.float32) * momentum_embeddings.astype(jnp.float32), axis=1
        )
        / contrastive_sharpness
    )
    larger = jnp.maximum(negative, matching_similarity)
    query_loss = (
        larger
        + jnp.log(jnp.exp(negative - larger) + jnp.exp(matching_similarity - larger))
        - matching_similarity
    )
    loss_sum = lax.psum(jnp.sum(query_loss), "dp")
    total_loss = loss_sum / (group_images * lax.axis_size("dp"))
    every_key = lax.all_gather(momentum_embeddings, "dp", axis=0, tiled=True)
    wanted = group_index * group_images + jnp.arange(group_images, dtype=jnp.int32)
    selector = (owner[None, :] == wanted[:, None]).astype(jnp.bfloat16)
    incoming_keys = jnp.dot(selector, every_key, preferred_element_type=jnp.float32).astype(
        jnp.bfloat16
    )
    row_place = section_index * share + jnp.arange(share, dtype=jnp.int32)
    slot_index = row_place - pointer[0]
    placing = (slot_index[:, None] == jnp.arange(group_images, dtype=jnp.int32)[None, :]).astype(
        jnp.bfloat16
    )
    written = jnp.dot(placing, incoming_keys, preferred_element_type=jnp.float32).astype(
        jnp.bfloat16
    )
    inside = jnp.logical_and(slot_index >= 0, slot_index < group_images)
    new_queue = jnp.where(inside[:, None], written, queue)
    return (momentum_embeddings, query_loss, total_loss, new_queue)


def solution(mesh):
    placed = (
        P("dp", None, None),
        P("section", None),
        P("section", None, None),
        P("section", None, None),
        P("section", None),
        P("section", None, None),
        P("section", None, None),
        P(),
        P(),
        P("dp", None),
        P(("dp", "section"), None),
        P(),
        P("dp"),
    )
    return jax.shard_map(
        on_device,
        mesh=mesh,
        in_specs=placed,
        out_specs=(P("dp", None), P("dp"), P(), P(("dp", "section"), None)),
        check_vma=False,
    )
```

```python
import functools
import math

import jax
import jax.numpy as jnp
from jax import lax
from jax.experimental import pallas as pl
from jax.experimental.pallas import tpu as pltpu
from jax.sharding import PartitionSpec as P

HEAD_DIM = 64


contrastive_sharpness = 0.2


def layer_norm(values, gain):
    center = values - jnp.mean(values, axis=-1, keepdims=True)
    spread = jnp.mean(center * center, axis=-1, keepdims=True)
    return center * lax.rsqrt(spread + 1e-06) * gain


def rounded_up(value, step):
    return (value + step - 1) // step * step


def gelu(x):
    return 0.5 * x * (1.0 + lax.erf(x * math.sqrt(0.5)))


def column_loop(total, tile, body):
    @pl.loop(0, total // tile)
    def _(step):
        body(pl.ds(pl.multiple_of(step * tile, tile), tile))


def attend(qkv_buf, c_buf, toks, width):
    rows = c_buf.shape[0]
    pair = 2 * HEAD_DIM
    lane = lax.broadcasted_iota(jnp.int32, (rows, pair), 1)
    first = lane < HEAD_DIM
    key_place = lax.broadcasted_iota(jnp.int32, (2 * rows, rows), 1)
    factor = math.log2(math.e) / math.sqrt(HEAD_DIM)

    def one_pair(columns, k_columns, v_columns):
        q = qkv_buf[:, columns]
        zero = jnp.zeros_like(q)
        q_both = jnp.concatenate([jnp.where(first, q, zero), jnp.where(first, zero, q)], axis=0)
        k = qkv_buf[:, k_columns]
        scores = lax.dot_general(
            q_both, k, (((1,), (1,)), ((), ())), preferred_element_type=jnp.float32
        )
        scores = jnp.where(key_place < toks, scores, -jnp.inf)
        peak = jnp.max(scores, axis=1, keepdims=True)
        expo = jnp.exp2((scores - peak) * factor)
        total = jnp.sum(expo, axis=1, keepdims=True)
        c = jnp.dot(
            expo.astype(jnp.bfloat16), qkv_buf[:, v_columns], preferred_element_type=jnp.float32
        )
        c = c / total
        c_buf[:, columns] = jnp.where(first, c[:rows], c[rows:]).astype(jnp.bfloat16)

    for at in range(0, width, pair):
        one_pair(
            pl.ds(at, pair),
            pl.ds(width + at, pair),
            pl.ds(2 * width + at, pair),
        )


def pipeline_kernel(
    sections,
    toks,
    groups,
    patches,
    online,
    gain_one,
    gain_two,
    w_qkv,
    w_out,
    w_fc1,
    w_fc2,
    class_rows,
    queries,
    v_qkv,
    v_out,
    v_fc1,
    v_fc2,
    raw,
    came,
    leaving,
    a_buf,
    qkv_buf,
    c_buf,
    r_buf,
    u_buf,
    weight_sem,
    raw_sem,
    send_sem,
    recv_sem,
    q_buf,
    q_send,
    q_recv,
):
    me = lax.axis_index("section")
    group = lax.axis_index("dp")
    images, rows, width = came.shape
    hidden_units = v_fc1.shape[1]
    loads = [
        pltpu.make_async_copy(source.at[0], target, weight_sem.at[place])
        for place, (source, target) in enumerate(
            ((w_qkv, v_qkv), (w_out, v_out), (w_fc1, v_fc1), (w_fc2, v_fc2))
        )
    ]

    def raw_load(image):
        return pltpu.make_async_copy(patches.at[image], raw.at[image], raw_sem.at[image])

    @pl.when(me == 0)
    def _():
        raw_load(0).start()

    loads[0].start()
    for load in loads[1:]:
        load.start()

    @pl.when(me == 0)
    def _():
        for image in range(1, images):
            raw_load(image).start()

    barrier = pltpu.get_barrier_semaphore()

    @pl.when(me > 0)
    def _():
        pl.semaphore_signal(
            barrier, inc=1, device_id={"section": me - 1}, device_id_type=pl.DeviceIdType.MESH
        )

    @pl.when(me < sections - 1)
    def _():
        pl.semaphore_signal(
            barrier, inc=1, device_id={"section": me + 1}, device_id_type=pl.DeviceIdType.MESH
        )

    for step in range(1, groups):
        pl.semaphore_signal(
            barrier,
            inc=1,
            device_id={"dp": lax.rem(group + step, groups)},
            device_id_type=pl.DeviceIdType.MESH,
        )

    inner = jnp.logical_and(me > 0, me < sections - 1)

    @pl.when(inner)
    def _():
        pl.semaphore_wait(barrier, groups + 1)

    @pl.when(jnp.logical_not(inner))
    def _():
        pl.semaphore_wait(barrier, groups)

    def query_copy(step):
        return pltpu.make_async_remote_copy(
            src_ref=online,
            dst_ref=q_buf.at[group],
            send_sem=q_send.at[step],
            recv_sem=q_recv.at[step],
            device_id={"dp": lax.rem(group + step, groups)},
            device_id_type=pl.DeviceIdType.MESH,
        )

    for step in range(1, groups):
        query_copy(step).start()

    def handing(image):
        return pltpu.make_async_remote_copy(
            src_ref=leaving.at[image],
            dst_ref=came.at[image],
            send_sem=send_sem.at[image],
            recv_sem=recv_sem.at[image],
            device_id={"section": jnp.minimum(me + 1, sections - 1)},
            device_id_type=pl.DeviceIdType.MESH,
        )

    @pl.loop(0, images)
    def _(image):
        @pl.when(me == 0)
        def _():
            raw_load(image).wait()
            came[image, toks // 16 * 16 :, :] = jnp.zeros(
                (rows - toks // 16 * 16, width), jnp.bfloat16
            )
            came[image, 0:toks, :] = raw[image]

        @pl.when(me > 0)
        def _():
            handing(image).wait_recv()

        def arrive(place):
            @pl.when(image == 0)
            def _():
                loads[place].wait()

        a_buf[...] = layer_norm(came[image].astype(jnp.float32), gain_one[...]).astype(jnp.bfloat16)
        arrive(0)

        def qkv_part(columns):
            qkv_buf[:, columns] = jnp.dot(
                a_buf[...], v_qkv[:, columns], preferred_element_type=jnp.float32
            ).astype(jnp.bfloat16)

        column_loop(3 * width, 512, qkv_part)
        attend(qkv_buf, c_buf, toks, width)
        arrive(1)

        def out_part(columns):
            r_buf[:, columns] = came[image, :, columns].astype(jnp.float32) + jnp.dot(
                c_buf[...], v_out[:, columns], preferred_element_type=jnp.float32
            )

        column_loop(width, 512, out_part)
        a_buf[...] = layer_norm(r_buf[...], gain_two[...]).astype(jnp.bfloat16)
        arrive(2)

        def fc1_part(columns):
            u_buf[:, columns] = gelu(
                jnp.dot(a_buf[...], v_fc1[:, columns], preferred_element_type=jnp.float32)
            ).astype(jnp.bfloat16)

        column_loop(hidden_units, 512, fc1_part)
        arrive(3)

        def fc2_part(columns):
            leaving[image, :, columns] = (
                r_buf[:, columns]
                + jnp.dot(u_buf[...], v_fc2[:, columns], preferred_element_type=jnp.float32)
            ).astype(jnp.bfloat16)

        column_loop(width, 512, fc2_part)

        @pl.when(me < sections - 1)
        def _():
            handing(image).start()

    for image in range(images):
        class_rows[image : image + 1, :] = leaving[image, 0:1, :]

    for step in range(1, groups):
        query_copy(step).wait()
    queries[...] = q_buf[...]
    queries[group] = online[...]

    @pl.when(me < sections - 1)
    def _():
        for image in range(images):
            handing(image).wait_send()


def run_pipeline(patches, online, gain_one, w_qkv, w_out, gain_two, w_fc1, w_fc2):
    sections = lax.axis_size("section")
    groups = lax.axis_size("dp")
    images, toks, width = patches.shape
    rows = rounded_up(toks, 16)
    hidden_units = w_fc1.shape[2]
    bf16 = jnp.bfloat16
    whole = pl.BlockSpec(memory_space=pltpu.VMEM)
    hbm = pl.BlockSpec(memory_space=pl.ANY)
    flops = 2 * images * toks * (4 * width * width + 2 * width * hidden_units)
    return pl.pallas_call(
        functools.partial(pipeline_kernel, sections, toks, groups),
        out_shape=(
            jax.ShapeDtypeStruct((images, width), bf16),
            jax.ShapeDtypeStruct((groups,) + online.shape, bf16),
        ),
        in_specs=[hbm, whole, whole, whole, hbm, hbm, hbm, hbm],
        out_specs=(whole, whole),
        scratch_shapes=[
            pltpu.VMEM((width, 3 * width), bf16),
            pltpu.VMEM((width, width), bf16),
            pltpu.VMEM((width, hidden_units), bf16),
            pltpu.VMEM((hidden_units, width), bf16),
            pltpu.VMEM((images, toks, width), bf16),
            pltpu.VMEM((images, rows, width), bf16),
            pltpu.VMEM((images, rows, width), bf16),
            pltpu.VMEM((rows, width), bf16),
            pltpu.VMEM((rows, 3 * width), bf16),
            pltpu.VMEM((rows, width), bf16),
            pltpu.VMEM((rows, width), jnp.float32),
            pltpu.VMEM((rows, hidden_units), bf16),
            pltpu.SemaphoreType.DMA((4,)),
            pltpu.SemaphoreType.DMA((images,)),
            pltpu.SemaphoreType.DMA((images,)),
            pltpu.SemaphoreType.DMA((images,)),
            pltpu.VMEM((groups,) + online.shape, bf16),
            pltpu.SemaphoreType.DMA((groups,)),
            pltpu.SemaphoreType.DMA((groups,)),
        ],
        compiler_params=pltpu.CompilerParams(
            collective_id=0, has_side_effects=True, vmem_limit_bytes=52 * 1024 * 1024
        ),
        cost_estimate=pl.CostEstimate(flops=flops, bytes_accessed=2**24, transcendentals=2**22),
    )(patches, online, gain_one, gain_two, w_qkv, w_out, w_fc1, w_fc2)


def exchange_kernel(groups, sections, mine, everyone, held, send_sem, recv_sem):
    group, me = lax.axis_index("dp"), lax.axis_index("section")
    place = group * sections + me
    peers = [
        {"dp": lax.rem(group + i, groups), "section": lax.rem(me + j, sections)}
        for i in range(groups)
        for j in range(sections)
    ][1:]
    barrier = pltpu.get_barrier_semaphore()
    for peer in peers:
        pl.semaphore_signal(barrier, inc=1, device_id=peer, device_id_type=pl.DeviceIdType.MESH)
    pl.semaphore_wait(barrier, len(peers))
    copies = [
        pltpu.make_async_remote_copy(
            src_ref=mine,
            dst_ref=held.at[place],
            send_sem=send_sem.at[turn],
            recv_sem=recv_sem.at[turn],
            device_id=peer,
            device_id_type=pl.DeviceIdType.MESH,
        )
        for turn, peer in enumerate(peers)
    ]
    for copy in copies:
        copy.start()
    for copy in copies:
        copy.wait()
    everyone[...] = held[...]
    everyone[place] = mine[...]


def exchange(mine):
    groups, sections = lax.axis_size("dp"), lax.axis_size("section")
    devices = groups * sections
    whole = pl.BlockSpec(memory_space=pltpu.VMEM)
    return pl.pallas_call(
        functools.partial(exchange_kernel, groups, sections),
        out_shape=jax.ShapeDtypeStruct((devices,) + mine.shape, mine.dtype),
        in_specs=[whole],
        out_specs=whole,
        scratch_shapes=[
            pltpu.VMEM((devices,) + mine.shape, mine.dtype),
            pltpu.SemaphoreType.DMA((devices,)),
            pltpu.SemaphoreType.DMA((devices,)),
        ],
        compiler_params=pltpu.CompilerParams(collective_id=1, has_side_effects=True),
    )(mine)


def key_head(class_rows, final_norm_gain, w_head):
    normed = layer_norm(class_rows.astype(jnp.float32), final_norm_gain).astype(jnp.bfloat16)
    projected = jnp.dot(normed, w_head, preferred_element_type=jnp.float32)
    scale = lax.rsqrt(1.0 + jnp.sum(projected * projected, axis=1, keepdims=True))
    return (projected * scale).astype(jnp.bfloat16)


def on_device(
    patches,
    ln1_gain,
    w_qkv,
    w_out,
    ln2_gain,
    w_fc1,
    w_fc2,
    final_norm_gain,
    w_head,
    online_embeddings,
    queue,
    owner,
    pointer,
):
    sections = lax.axis_size("section")
    section_index = lax.axis_index("section")
    group_index = lax.axis_index("dp")
    group_images = patches.shape[0]
    groups = lax.axis_size("dp")
    finished, query_blocks = run_pipeline(
        patches, online_embeddings, ln1_gain, w_qkv, w_out, ln2_gain, w_fc1, w_fc2
    )
    kdim = online_embeddings.shape[1]
    query_rows_full = query_blocks.reshape(groups * group_images, kdim)
    resident_embeddings = key_head(finished, final_norm_gain, w_head)
    share = queue.shape[0]
    similarity_matrix = (
        jnp.einsum("tw,fw->tf", query_rows_full, queue, preferred_element_type=jnp.float32)
        / contrastive_sharpness
    )
    local_peak = jnp.max(similarity_matrix, axis=1)
    local_total = jnp.sum(jnp.exp(similarity_matrix - local_peak[:, None]), axis=1)
    used = kdim + 2 * groups
    message = jnp.concatenate(
        [
            resident_embeddings.astype(jnp.float32),
            local_peak.reshape(groups, group_images).T,
            local_total.reshape(groups, group_images).T,
            jnp.zeros((group_images, rounded_up(used, 128) - used), jnp.float32),
        ],
        axis=1,
    )
    told = exchange(message)
    every_key = told.reshape(groups, sections, group_images, -1)[:, sections - 1, :, :kdim]
    every_key = every_key.reshape(groups * group_images, kdim).astype(jnp.bfloat16)
    momentum_embeddings = lax.dynamic_slice_in_dim(
        every_key, group_index * group_images, group_images, 0
    )
    peaks = told[:, :, kdim : kdim + groups]
    totals = told[:, :, kdim + groups : kdim + 2 * groups]
    top = jnp.max(peaks, axis=0)
    total = jnp.sum(totals * jnp.exp(peaks - top[None]), axis=0)
    negative = (top + jnp.log(total)).T
    matching_similarity = (
        jnp.sum(query_rows_full.astype(jnp.float32) * every_key.astype(jnp.float32), axis=1)
        / contrastive_sharpness
    ).reshape(groups, group_images)
    larger = jnp.maximum(negative, matching_similarity)
    every_loss = (
        larger
        + jnp.log(jnp.exp(negative - larger) + jnp.exp(matching_similarity - larger))
        - matching_similarity
    )
    query_loss = lax.dynamic_index_in_dim(every_loss, group_index, 0, keepdims=False)
    total_loss = jnp.sum(every_loss) / (group_images * groups)
    wanted = group_index * group_images + jnp.arange(group_images, dtype=jnp.int32)
    selector = (owner[None, :] == wanted[:, None]).astype(jnp.bfloat16)
    incoming_keys = jnp.dot(selector, every_key, preferred_element_type=jnp.float32).astype(
        jnp.bfloat16
    )
    row_place = section_index * share + jnp.arange(share, dtype=jnp.int32)
    slot_index = row_place - pointer[0]
    placing = (slot_index[:, None] == jnp.arange(group_images, dtype=jnp.int32)[None, :]).astype(
        jnp.bfloat16
    )
    written = jnp.dot(placing, incoming_keys, preferred_element_type=jnp.float32).astype(
        jnp.bfloat16
    )
    inside = jnp.logical_and(slot_index >= 0, slot_index < group_images)
    new_queue = jnp.where(inside[:, None], written, queue)
    return (momentum_embeddings, query_loss, total_loss, new_queue)


def solution(mesh):
    placed = (
        P("dp", None, None),
        P("section", None),
        P("section", None, None),
        P("section", None, None),
        P("section", None),
        P("section", None, None),
        P("section", None, None),
        P(),
        P(),
        P("dp", None),
        P(("dp", "section"), None),
        P(),
        P("dp"),
    )
    return jax.shard_map(
        on_device,
        mesh=mesh,
        in_specs=placed,
        out_specs=(P("dp", None), P("dp"), P(), P(("dp", "section"), None)),
        check_vma=False,
    )
```

```python
import functools
import math

import jax
import jax.numpy as jnp
from jax import lax
from jax.experimental import pallas as pl
from jax.experimental.pallas import tpu as pltpu
from jax.sharding import PartitionSpec as P

HEAD_DIM = 64


contrastive_sharpness = 0.2


def layer_norm(values, gain):
    center = values - jnp.mean(values, axis=-1, keepdims=True)
    spread = jnp.mean(center * center, axis=-1, keepdims=True)
    return center * lax.rsqrt(spread + 1e-06) * gain


def rounded_up(value, step):
    return (value + step - 1) // step * step


def gelu(x):
    return 0.5 * x * (1.0 + lax.erf(x * math.sqrt(0.5)))


def column_loop(total, tile, body):
    for at in range(0, total, tile):
        body(pl.ds(at, tile))


def attend(qkv_buf, c_buf, toks, width):
    rows = c_buf.shape[0]
    pair = 2 * HEAD_DIM
    lane = lax.broadcasted_iota(jnp.int32, (rows, pair), 1)
    first = lane < HEAD_DIM
    key_place = lax.broadcasted_iota(jnp.int32, (2 * rows, rows), 1)
    factor = math.log2(math.e) / math.sqrt(HEAD_DIM)

    def one_pair(columns, k_columns, v_columns):
        q = qkv_buf[:, columns]
        zero = jnp.zeros_like(q)
        q_both = jnp.concatenate([jnp.where(first, q, zero), jnp.where(first, zero, q)], axis=0)
        k = qkv_buf[:, k_columns]
        scores = lax.dot_general(
            q_both, k, (((1,), (1,)), ((), ())), preferred_element_type=jnp.float32
        )
        scores = jnp.where(key_place < toks, scores, -jnp.inf)
        peak = jnp.max(scores, axis=1, keepdims=True)
        expo = jnp.exp2((scores - peak) * factor)
        v = qkv_buf[:, v_columns]
        v_and_one = jnp.concatenate([v, jnp.ones_like(v)], axis=1)
        c = jnp.dot(expo.astype(jnp.bfloat16), v_and_one, preferred_element_type=jnp.float32)
        above = jnp.where(first, c[:rows, :pair], c[rows:, :pair])
        below = jnp.where(first, c[:rows, pair:], c[rows:, pair:])
        c_buf[:, columns] = (above / below).astype(jnp.bfloat16)

    for at in range(0, width, pair):
        one_pair(
            pl.ds(at, pair),
            pl.ds(width + at, pair),
            pl.ds(2 * width + at, pair),
        )


def pipeline_kernel(
    sections,
    toks,
    groups,
    patches,
    online,
    gain_one,
    gain_two,
    w_qkv,
    w_out,
    w_fc1,
    w_fc2,
    class_rows,
    queries,
    v_qkv,
    v_out,
    v_fc1,
    v_fc2,
    raw,
    came,
    leaving,
    a_buf,
    qkv_buf,
    c_buf,
    r_buf,
    u_buf,
    weight_sem,
    raw_sem,
    send_sem,
    recv_sem,
    q_buf,
    q_send,
    q_recv,
):
    me = lax.axis_index("section")
    group = lax.axis_index("dp")
    images, rows, width = came.shape
    hidden_units = v_fc1.shape[1]
    loads = [
        pltpu.make_async_copy(source.at[0], target, weight_sem.at[place])
        for place, (source, target) in enumerate(
            ((w_qkv, v_qkv), (w_out, v_out), (w_fc1, v_fc1), (w_fc2, v_fc2))
        )
    ]

    def raw_load(image):
        return pltpu.make_async_copy(patches.at[image], raw.at[image], raw_sem.at[image])

    @pl.when(me == 0)
    def _():
        raw_load(0).start()

    loads[0].start()
    for load in loads[1:]:
        load.start()

    @pl.when(me == 0)
    def _():
        for image in range(1, images):
            raw_load(image).start()

    barrier = pltpu.get_barrier_semaphore()

    @pl.when(me > 0)
    def _():
        pl.semaphore_signal(
            barrier, inc=1, device_id={"section": me - 1}, device_id_type=pl.DeviceIdType.MESH
        )

    @pl.when(me < sections - 1)
    def _():
        pl.semaphore_signal(
            barrier, inc=1, device_id={"section": me + 1}, device_id_type=pl.DeviceIdType.MESH
        )

    for step in range(1, groups):
        pl.semaphore_signal(
            barrier,
            inc=1,
            device_id={"dp": lax.rem(group + step, groups)},
            device_id_type=pl.DeviceIdType.MESH,
        )

    inner = jnp.logical_and(me > 0, me < sections - 1)

    @pl.when(inner)
    def _():
        pl.semaphore_wait(barrier, groups + 1)

    @pl.when(jnp.logical_not(inner))
    def _():
        pl.semaphore_wait(barrier, groups)

    def query_copy(step):
        return pltpu.make_async_remote_copy(
            src_ref=online,
            dst_ref=q_buf.at[group],
            send_sem=q_send.at[step],
            recv_sem=q_recv.at[step],
            device_id={"dp": lax.rem(group + step, groups)},
            device_id_type=pl.DeviceIdType.MESH,
        )

    for step in range(1, groups):
        query_copy(step).start()

    def handing(image):
        return pltpu.make_async_remote_copy(
            src_ref=leaving.at[image],
            dst_ref=came.at[image],
            send_sem=send_sem.at[image],
            recv_sem=recv_sem.at[image],
            device_id={"section": jnp.minimum(me + 1, sections - 1)},
            device_id_type=pl.DeviceIdType.MESH,
        )

    @pl.loop(0, images)
    def _(image):
        @pl.when(me == 0)
        def _():
            raw_load(image).wait()
            came[image, toks // 16 * 16 :, :] = jnp.zeros(
                (rows - toks // 16 * 16, width), jnp.bfloat16
            )
            came[image, 0:toks, :] = raw[image]

        @pl.when(me > 0)
        def _():
            handing(image).wait_recv()

        def arrive(place):
            @pl.when(image == 0)
            def _():
                loads[place].wait()

        a_buf[...] = layer_norm(came[image].astype(jnp.float32), gain_one[...]).astype(jnp.bfloat16)
        arrive(0)

        def qkv_part(columns):
            qkv_buf[:, columns] = jnp.dot(
                a_buf[...], v_qkv[:, columns], preferred_element_type=jnp.float32
            ).astype(jnp.bfloat16)

        column_loop(3 * width, 512, qkv_part)
        attend(qkv_buf, c_buf, toks, width)
        arrive(1)

        def out_part(columns):
            r_buf[:, columns] = came[image, :, columns].astype(jnp.float32) + jnp.dot(
                c_buf[...], v_out[:, columns], preferred_element_type=jnp.float32
            )

        column_loop(width, 512, out_part)
        a_buf[...] = layer_norm(r_buf[...], gain_two[...]).astype(jnp.bfloat16)
        arrive(2)

        def fc1_part(columns):
            u_buf[:, columns] = gelu(
                jnp.dot(a_buf[...], v_fc1[:, columns], preferred_element_type=jnp.float32)
            ).astype(jnp.bfloat16)

        column_loop(hidden_units, 512, fc1_part)
        arrive(3)

        def fc2_part(columns):
            leaving[image, :, columns] = (
                r_buf[:, columns]
                + jnp.dot(u_buf[...], v_fc2[:, columns], preferred_element_type=jnp.float32)
            ).astype(jnp.bfloat16)

        column_loop(width, 512, fc2_part)

        @pl.when(me < sections - 1)
        def _():
            handing(image).start()

    for image in range(images):
        class_rows[image : image + 1, :] = leaving[image, 0:1, :]

    for step in range(1, groups):
        query_copy(step).wait()
    queries[...] = q_buf[...]
    queries[group] = online[...]

    @pl.when(me < sections - 1)
    def _():
        for image in range(images):
            handing(image).wait_send()


def run_pipeline(patches, online, gain_one, w_qkv, w_out, gain_two, w_fc1, w_fc2):
    sections = lax.axis_size("section")
    groups = lax.axis_size("dp")
    images, toks, width = patches.shape
    rows = rounded_up(toks, 16)
    hidden_units = w_fc1.shape[2]
    bf16 = jnp.bfloat16
    whole = pl.BlockSpec(memory_space=pltpu.VMEM)
    hbm = pl.BlockSpec(memory_space=pl.ANY)
    flops = 2 * images * toks * (4 * width * width + 2 * width * hidden_units)
    return pl.pallas_call(
        functools.partial(pipeline_kernel, sections, toks, groups),
        out_shape=(
            jax.ShapeDtypeStruct((images, width), bf16),
            jax.ShapeDtypeStruct((groups,) + online.shape, bf16),
        ),
        in_specs=[hbm, whole, whole, whole, hbm, hbm, hbm, hbm],
        out_specs=(whole, whole),
        scratch_shapes=[
            pltpu.VMEM((width, 3 * width), bf16),
            pltpu.VMEM((width, width), bf16),
            pltpu.VMEM((width, hidden_units), bf16),
            pltpu.VMEM((hidden_units, width), bf16),
            pltpu.VMEM((images, toks, width), bf16),
            pltpu.VMEM((images, rows, width), bf16),
            pltpu.VMEM((images, rows, width), bf16),
            pltpu.VMEM((rows, width), bf16),
            pltpu.VMEM((rows, 3 * width), bf16),
            pltpu.VMEM((rows, width), bf16),
            pltpu.VMEM((rows, width), jnp.float32),
            pltpu.VMEM((rows, hidden_units), bf16),
            pltpu.SemaphoreType.DMA((4,)),
            pltpu.SemaphoreType.DMA((images,)),
            pltpu.SemaphoreType.DMA((images,)),
            pltpu.SemaphoreType.DMA((images,)),
            pltpu.VMEM((groups,) + online.shape, bf16),
            pltpu.SemaphoreType.DMA((groups,)),
            pltpu.SemaphoreType.DMA((groups,)),
        ],
        compiler_params=pltpu.CompilerParams(
            collective_id=0, has_side_effects=True, vmem_limit_bytes=52 * 1024 * 1024
        ),
        cost_estimate=pl.CostEstimate(flops=flops, bytes_accessed=2**24, transcendentals=2**22),
    )(patches, online, gain_one, gain_two, w_qkv, w_out, w_fc1, w_fc2)


def exchange_kernel(groups, sections, mine, everyone, held, send_sem, recv_sem):
    group, me = lax.axis_index("dp"), lax.axis_index("section")
    place = group * sections + me
    peers = [
        {"dp": lax.rem(group + i, groups), "section": lax.rem(me + j, sections)}
        for i in range(groups)
        for j in range(sections)
    ][1:]
    barrier = pltpu.get_barrier_semaphore()
    for peer in peers:
        pl.semaphore_signal(barrier, inc=1, device_id=peer, device_id_type=pl.DeviceIdType.MESH)
    pl.semaphore_wait(barrier, len(peers))
    copies = [
        pltpu.make_async_remote_copy(
            src_ref=mine,
            dst_ref=held.at[place],
            send_sem=send_sem.at[turn],
            recv_sem=recv_sem.at[turn],
            device_id=peer,
            device_id_type=pl.DeviceIdType.MESH,
        )
        for turn, peer in enumerate(peers)
    ]
    for copy in copies:
        copy.start()
    for copy in copies:
        copy.wait()
    everyone[...] = held[...]
    everyone[place] = mine[...]


def exchange(mine):
    groups, sections = lax.axis_size("dp"), lax.axis_size("section")
    devices = groups * sections
    whole = pl.BlockSpec(memory_space=pltpu.VMEM)
    return pl.pallas_call(
        functools.partial(exchange_kernel, groups, sections),
        out_shape=jax.ShapeDtypeStruct((devices,) + mine.shape, mine.dtype),
        in_specs=[whole],
        out_specs=whole,
        scratch_shapes=[
            pltpu.VMEM((devices,) + mine.shape, mine.dtype),
            pltpu.SemaphoreType.DMA((devices,)),
            pltpu.SemaphoreType.DMA((devices,)),
        ],
        compiler_params=pltpu.CompilerParams(collective_id=1, has_side_effects=True),
    )(mine)


def key_head(class_rows, final_norm_gain, w_head):
    normed = layer_norm(class_rows.astype(jnp.float32), final_norm_gain).astype(jnp.bfloat16)
    projected = jnp.dot(normed, w_head, preferred_element_type=jnp.float32)
    scale = lax.rsqrt(1.0 + jnp.sum(projected * projected, axis=1, keepdims=True))
    return (projected * scale).astype(jnp.bfloat16)


def on_device(
    patches,
    ln1_gain,
    w_qkv,
    w_out,
    ln2_gain,
    w_fc1,
    w_fc2,
    final_norm_gain,
    w_head,
    online_embeddings,
    queue,
    owner,
    pointer,
):
    sections = lax.axis_size("section")
    section_index = lax.axis_index("section")
    group_index = lax.axis_index("dp")
    group_images = patches.shape[0]
    groups = lax.axis_size("dp")
    finished, query_blocks = run_pipeline(
        patches, online_embeddings, ln1_gain, w_qkv, w_out, ln2_gain, w_fc1, w_fc2
    )
    kdim = online_embeddings.shape[1]
    query_rows_full = query_blocks.reshape(groups * group_images, kdim)
    resident_embeddings = key_head(finished, final_norm_gain, w_head)
    share = queue.shape[0]
    similarity_matrix = (
        jnp.einsum("tw,fw->tf", query_rows_full, queue, preferred_element_type=jnp.float32)
        / contrastive_sharpness
    )
    local_peak = jnp.max(similarity_matrix, axis=1)
    local_total = jnp.sum(jnp.exp(similarity_matrix - local_peak[:, None]), axis=1)
    used = kdim + 2 * groups
    message = jnp.concatenate(
        [
            resident_embeddings.astype(jnp.float32),
            local_peak.reshape(groups, group_images).T,
            local_total.reshape(groups, group_images).T,
            jnp.zeros((group_images, rounded_up(used, 128) - used), jnp.float32),
        ],
        axis=1,
    )
    told = exchange(message)
    every_key = told.reshape(groups, sections, group_images, -1)[:, sections - 1, :, :kdim]
    every_key = every_key.reshape(groups * group_images, kdim).astype(jnp.bfloat16)
    momentum_embeddings = lax.dynamic_slice_in_dim(
        every_key, group_index * group_images, group_images, 0
    )
    peaks = told[:, :, kdim : kdim + groups]
    totals = told[:, :, kdim + groups : kdim + 2 * groups]
    top = jnp.max(peaks, axis=0)
    total = jnp.sum(totals * jnp.exp(peaks - top[None]), axis=0)
    negative = (top + jnp.log(total)).T
    matching_similarity = (
        jnp.sum(query_rows_full.astype(jnp.float32) * every_key.astype(jnp.float32), axis=1)
        / contrastive_sharpness
    ).reshape(groups, group_images)
    larger = jnp.maximum(negative, matching_similarity)
    every_loss = (
        larger
        + jnp.log(jnp.exp(negative - larger) + jnp.exp(matching_similarity - larger))
        - matching_similarity
    )
    query_loss = lax.dynamic_index_in_dim(every_loss, group_index, 0, keepdims=False)
    total_loss = jnp.sum(every_loss) / (group_images * groups)
    wanted = group_index * group_images + jnp.arange(group_images, dtype=jnp.int32)
    selector = (owner[None, :] == wanted[:, None]).astype(jnp.bfloat16)
    incoming_keys = jnp.dot(selector, every_key, preferred_element_type=jnp.float32).astype(
        jnp.bfloat16
    )
    row_place = section_index * share + jnp.arange(share, dtype=jnp.int32)
    slot_index = row_place - pointer[0]
    placing = (slot_index[:, None] == jnp.arange(group_images, dtype=jnp.int32)[None, :]).astype(
        jnp.bfloat16
    )
    written = jnp.dot(placing, incoming_keys, preferred_element_type=jnp.float32).astype(
        jnp.bfloat16
    )
    inside = jnp.logical_and(slot_index >= 0, slot_index < group_images)
    new_queue = jnp.where(inside[:, None], written, queue)
    return (momentum_embeddings, query_loss, total_loss, new_queue)


def solution(mesh):
    placed = (
        P("dp", None, None),
        P("section", None),
        P("section", None, None),
        P("section", None, None),
        P("section", None),
        P("section", None, None),
        P("section", None, None),
        P(),
        P(),
        P("dp", None),
        P(("dp", "section"), None),
        P(),
        P("dp"),
    )
    return jax.shard_map(
        on_device,
        mesh=mesh,
        in_specs=placed,
        out_specs=(P("dp", None), P("dp"), P(), P(("dp", "section"), None)),
        check_vma=False,
    )
```
